256 devices in a mesh: tm: 32 (over y_hi, z, core), head: 8 (over y_lo, x).
Axes of the slice: x: 4, y: 4 (y_hi: 2, y_lo: 2; y = y_hi * 2 + y_lo), z: 8, core: 2. Of those that a mesh axis runs over, the one named last changes fastest.
Arguments:
- frames: bfloat16 [16384, 1024], P('tm'), may hold values from -8 to 8
- norm_gain: float32 [1024], replicated, may hold values from 0.5 to 1.5
- w_qkv: bfloat16 [3, 1024, 1024], P(None, 'tm', 'head'), may hold values from -6 to 6
- slopes: float32 [8], P('head'), may hold values from 1.5258789e-05 to 0.05
- w_out: bfloat16 [1024, 1024], P('head', 'tm'), may hold values from -0.5 to 0.5
Outputs:
- attended: bfloat16 [16384, 1024], P(('tm', 'head'))
The draws below stay inside these ranges and needn't reach their ends.
All inputs are finite; a program needn't handle non-finite values.
Results may differ from the reference program's by a relative error of at most 0.014.
Values may be sent and summed in bfloat16 or wider, within the bound.
No kernel may reach another device: no remote copies, remote signals or barrier semaphores. Data moves between devices by JAX's collectives and lax.ppermute only.
A program may use at most 128 MiB of HBM per device.

```python
import math
import jax
import jax.numpy as jnp
from jax import lax

D = 1024
H = 8
HD = 128
FR_DEV = 512
L = 16384


def draw_frames(key, part):
    first = jax.random.fold_in(key, 0)
    values = jax.random.normal(first, (L, D), jnp.float32)
    return jnp.clip(values, -8.0, 8.0).astype(jnp.bfloat16)


def draw_w_qkv(key, part):
    first, second, third = jax.random.split(key, 3)
    inverse = D ** (-0.5)
    w_query = jax.random.normal(first, (D, D), jnp.float32) * inverse
    w_key = jax.random.normal(second, (D, D), jnp.float32) * inverse
    w_value = jax.random.normal(third, (D, D), jnp.float32) * inverse
    stacked = jnp.stack([w_query, w_key, w_value], axis=0)
    return jnp.clip(stacked, -6.0, 6.0).astype(jnp.bfloat16)


def block_scale(rng, extent, pieces, smallest, top_value):
    level, own = 1.0, jax.random.fold_in(rng, 6)
    for dim, parts in pieces:
        heights = jnp.exp(jax.random.uniform(jax.random.fold_in(own, dim), (parts,), jnp.float32, smallest / len(pieces), top_value / len(pieces)))
        level = level * jnp.repeat(heights, extent[dim] // parts).reshape([-1 if axis == dim else 1 for axis in range(len(extent))])
    return level


def normal_values(key, shape, width, reach, cuts=(), kind=jnp.bfloat16):
    entries = width * jax.random.normal(key, shape, jnp.float32)
    if cuts:
        entries = entries * block_scale(key, shape, cuts, -0.22, 0.18)
    return jnp.clip(entries, -reach, reach).astype(kind)


def setup_inputs(seed: int = 0) -> dict:
    key_list = jax.random.split(jax.random.key(seed), 6)
    frames = draw_frames(jax.random.fold_in(key_list[5], 71), 0)
    norm_gain = jnp.clip(1.0 + 0.1 * jax.random.normal(key_list[1], (D,), jnp.float32), 0.5, 1.5)
    w_qkv = draw_w_qkv(jax.random.fold_in(key_list[5], 71), 0)
    slopes = jnp.clip(jnp.exp(math.log(0.05) - 8.094623 * jax.random.uniform(key_list[3], (H,), jnp.float32) ** block_scale(key_list[3], (H,), ((0, 8),), -0.2, 0.2)), 1.52587890625e-05, 0.05)
    w_out = normal_values(key_list[4], (D, D), HD ** -0.5, 0.5, ((0, 8), (1, 32)))
    return {"frames": frames, "norm_gain": norm_gain, "w_qkv": w_qkv, "slopes": slopes, "w_out": w_out}


def reference(frames, norm_gain, w_qkv, slopes, w_out):
    wide = frames.astype(jnp.float32)
    mean_square = lax.optimization_barrier(jnp.mean(wide * wide, axis=-1, keepdims=True))
    inverse_root = lax.rsqrt(mean_square + 1e-06)
    normed = (wide * inverse_root * norm_gain).astype(jnp.bfloat16)
    query = jnp.dot(normed, w_qkv[0], preferred_element_type=jnp.float32).astype(jnp.bfloat16).reshape(L, H, HD)
    keyed = jnp.dot(normed, w_qkv[1], preferred_element_type=jnp.float32).astype(jnp.bfloat16).reshape(L, H, HD)
    valued = jnp.dot(normed, w_qkv[2], preferred_element_type=jnp.float32).astype(jnp.bfloat16).reshape(L, H, HD)
    key_wide = keyed.astype(jnp.float32)
    value_wide = valued.astype(jnp.float32)
    block = FR_DEV if FR_DEV <= 512 else 512
    count = L // block
    scale = HD ** (-0.5)
    columns = jnp.arange(L, dtype=jnp.int32)

    def one_block(index):
        start = (index * block).astype(jnp.int32)
        query_block = lax.dynamic_slice_in_dim(query, start, block, 0).astype(jnp.float32)
        scores = jnp.einsum('qhd,khd->hqk', query_block, key_wide, precision=lax.Precision.HIGHEST) * scale
        rows_now = start + jnp.arange(block, dtype=jnp.int32)
        differ = (columns[None, :] - rows_now[:, None]) % L
        distance = jnp.minimum(differ, L - differ).astype(jnp.float32)
        scores = scores - slopes[:, None, None] * distance[None, :, :]
        peak = lax.optimization_barrier(jnp.max(scores, axis=-1, keepdims=True))
        expo = jnp.exp(scores - peak)
        totals = lax.optimization_barrier(jnp.sum(expo, axis=-1))
        weights = expo.astype(jnp.bfloat16).astype(jnp.float32)
        numer = jnp.einsum('hqk,khd->qhd', weights, value_wide, precision=lax.Precision.HIGHEST)
        mixed = numer / jnp.transpose(totals)[:, :, None]
        return mixed.astype(jnp.bfloat16).reshape(block, H * HD)
    mixed = lax.map(one_block, jnp.arange(count, dtype=jnp.int32)).reshape(L, H * HD)
    return jnp.dot(mixed, w_out, preferred_element_type=jnp.float32).astype(jnp.bfloat16)
```

```python
import functools
import math

import jax
import jax.numpy as jnp
from jax import lax
from jax.experimental import pallas as pl
from jax.experimental.pallas import tpu as pltpu
from jax.sharding import PartitionSpec as P

F32, BF16 = jnp.float32, jnp.bfloat16
LOG2E = math.log2(math.e)
YH, Z, CORE = 2, 8, 2
TM = YH * Z * CORE


def tm_permute(x, d_yh, d_z, d_core):
    pairs = []
    for yh in range(YH):
        for z in range(Z):
            for core in range(CORE):
                source = ((yh + d_yh) % YH * Z + (z + d_z) % Z) * CORE + (core + d_core) % CORE
                pairs.append((source, (yh * Z + z) * CORE + core))
    return lax.ppermute(x, "tm", pairs)


def split_bf16(x):
    high = x.astype(BF16)
    rest = x - high.astype(F32)
    mid = rest.astype(BF16)
    return high, mid, (rest - mid.astype(F32)).astype(BF16)


def pack_partial(out, lse):
    high, mid, low = split_bf16(lse)
    lane = lax.broadcasted_iota(jnp.int32, lse.shape, 1)
    stat = jnp.where(lane < 32, high.astype(F32), jnp.where(lane < 64, mid.astype(F32), low.astype(F32)))
    return jnp.concatenate([out.astype(BF16), stat.astype(BF16)], axis=1)


def unpack_partial(packed):
    out = packed[:, :128].astype(F32)
    stat = packed[:, 128:].astype(F32)
    lse = stat[:, 0:1] + stat[:, 32:33] + stat[:, 64:65]
    return out, jnp.broadcast_to(lse, out.shape)


def attention_kernel(shards, offset, first, last, scale, *refs):
    kind_ref, base_ref = refs[:2]
    q_ref = refs[2]
    kv_refs = refs[3 : 3 + shards]
    bias_refs = refs[3 + shards : 3 + 2 * shards]
    rest = refs[3 + 2 * shards :]
    if not first:
        peak_ref, sums_ref = rest[:2]
        rest = rest[2:]
    out_refs = rest
    block = pl.program_id(0)
    rows = q_ref.shape[0]
    keys = kv_refs[0].shape[0]
    chunk = 256
    ones = jnp.ones((keys, 128), BF16)
    bases = [base_ref[offset + 4 * j + block] for j in range(shards)]
    for start in range(0, rows, chunk):
        here = pl.ds(start, chunk)
        query = q_ref[here, :]
        scores, top = [], None
        for j in range(shards):
            score = lax.dot_general(
                query, kv_refs[j][:, :128], (((1,), (1,)), ((), ())), preferred_element_type=F32
            )
            score = score * scale + bias_refs[j][0, here, :]
            scores.append(score)
            here_top = jnp.max(score, axis=1, keepdims=True) - bases[j]
            top = here_top if top is None else jnp.maximum(top, here_top)
        peak = jnp.broadcast_to(top, (chunk, 128))
        if not first:
            old = peak_ref[here, :]
            peak = jnp.maximum(peak, old)
        total = None
        for j in range(shards):
            weight = jnp.exp2(scores[j] - jnp.tile(peak + bases[j], (1, keys // 128))).astype(BF16)
            value = jnp.concatenate([kv_refs[j][:, 128:], ones], axis=1)
            part = jnp.dot(weight, value, preferred_element_type=F32)
            total = part if total is None else total + part
        if not first:
            total = total + sums_ref[here, :] * jnp.tile(jnp.exp2(old - peak), (1, 2))
        if last:
            norm = total[:, :128] / total[:, 128:]
            lse = peak + jnp.log2(total[:, 128:])
            out_refs[0][here, :] = pack_partial(norm, lse)
            out_refs[1][here, :] = norm
            out_refs[2][here, :] = lse
        else:
            out_refs[0][here, :] = peak
            out_refs[1][here, :] = total


def attention_step(kinds, bases, query, kvs, bias, state, first_shard, last, scale):
    shards = len(kvs)
    total_rows = query.shape[0]
    keys = kvs[0].shape[0]
    rows = bias.shape[1]
    first = state is None
    offset = 4 * first_shard
    in_specs = [pl.BlockSpec((rows, 128), lambda i, kind, base: (i, 0))]
    in_specs += [pl.BlockSpec((keys, 256), lambda i, kind, base: (0, 0)) for _ in kvs]
    for j in range(shards):
        in_specs.append(
            pl.BlockSpec((1, rows, keys), lambda i, kind, base, j=j: (kind[offset + 4 * j + i], 0, 0))
        )
    args = [kinds, bases, query, *kvs] + [bias] * shards
    if not first:
        in_specs += [
            pl.BlockSpec((rows, 128), lambda i, kind, base: (i, 0)),
            pl.BlockSpec((rows, 256), lambda i, kind, base: (i, 0)),
        ]
        args += list(state)
    if last:
        shapes = [((total_rows, 256), BF16), ((total_rows, 128), F32), ((total_rows, 128), F32)]
    else:
        shapes = [((total_rows, 128), F32), ((total_rows, 256), F32)]
    out_specs = [pl.BlockSpec((rows, s[1]), lambda i, kind, base: (i, 0)) for s, _ in shapes]
    return pl.pallas_call(
        functools.partial(attention_kernel, shards, offset, first, last, scale),
        out_shape=[jax.ShapeDtypeStruct(s, t) for s, t in shapes],
        grid_spec=pltpu.PrefetchScalarGridSpec(
            num_scalar_prefetch=2,
            grid=(total_rows // rows,),
            in_specs=in_specs,
            out_specs=out_specs,
        ),
        cost_estimate=pl.CostEstimate(
            flops=4 * total_rows * keys * shards * 256,
            bytes_accessed=total_rows * 3072 + shards * keys * 512,
            transcendentals=total_rows * keys * shards,
        ),
    )(*args)


def merge(out_a, lse_a, out_b, lse_b):
    top = jnp.maximum(lse_a, lse_b)
    part_a, part_b = jnp.exp2(lse_a - top), jnp.exp2(lse_b - top)
    both = part_a + part_b
    return (out_a * part_a + out_b * part_b) / both, top + jnp.log2(both)


def merge_core_kernel(out_ref, lse_ref, got_ref, send_ref, keep_ref, keep_lse_ref):
    block = pl.program_id(0)
    got, got_lse = unpack_partial(got_ref[...])
    out, lse = merge(out_ref[...], lse_ref[...], got, got_lse)

    @pl.when(block == 0)
    def _():
        keep_ref[...] = out
        keep_lse_ref[...] = lse

    @pl.when(block == 1)
    def _():
        send_ref[...] = pack_partial(out, lse)


def merge_core(out, lse, got, rows):
    row_block = lambda i: (i, 0)
    fixed = lambda i: (0, 0)
    return pl.pallas_call(
        merge_core_kernel,
        out_shape=[
            jax.ShapeDtypeStruct((rows, 256), BF16),
            jax.ShapeDtypeStruct((rows, 128), F32),
            jax.ShapeDtypeStruct((rows, 128), F32),
        ],
        grid=(2,),
        in_specs=[
            pl.BlockSpec((rows, 128), row_block),
            pl.BlockSpec((rows, 128), row_block),
            pl.BlockSpec((rows, 256), row_block),
        ],
        out_specs=[
            pl.BlockSpec((rows, 256), fixed),
            pl.BlockSpec((rows, 128), fixed),
            pl.BlockSpec((rows, 128), fixed),
        ],
    )(out, lse, got)


def merge_project_kernel(out_ref, lse_ref, got_ref, w_ref, partial_ref):
    got, got_lse = unpack_partial(got_ref[...])
    out, _ = merge(out_ref[...], lse_ref[...], got, got_lse)
    partial_ref[...] = lax.dot_general(
        out.astype(BF16), w_ref[...], (((1,), (1,)), ((), ())), preferred_element_type=F32
    ).astype(BF16)


def merge_project(out, lse, got, w_out_t):
    rows, width = out.shape[0], w_out_t.shape[0]
    return pl.pallas_call(
        merge_project_kernel,
        out_shape=jax.ShapeDtypeStruct((rows, width), BF16),
    )(out, lse, got, w_out_t)


def local(frames, norm_gain, w_qkv, slopes, w_out):
    rows, width = frames.shape
    me = lax.axis_index("tm")
    core, z, yh = me % CORE, me // CORE % Z, me // (CORE * Z)

    part = w_qkv.shape[1]
    own = jnp.concatenate([w_qkv.reshape(3 * part, 128), w_out.T], axis=0)
    held = jnp.zeros((Z,) + own.shape, BF16)
    held = lax.dynamic_update_slice(held, own[None], (z, 0, 0))
    up = down = own
    for step in range(1, Z // 2 + 1):
        up = tm_permute(up, 0, 1, 0)
        held = lax.dynamic_update_slice(held, up[None], ((z + step) % Z, 0, 0))
        if step < Z // 2:
            down = tm_permute(down, 0, -1, 0)
            held = lax.dynamic_update_slice(held, down[None], ((z - step) % Z, 0, 0))
    other = tm_permute(held, 1, 0, 0)
    flip = yh == 1
    held = jnp.stack([jnp.where(flip, other, held), jnp.where(flip, held, other)])
    other = tm_permute(held, 0, 0, 1)
    flip = core == 1
    held = jnp.stack([jnp.where(flip, other, held), jnp.where(flip, held, other)], axis=2)
    held = held.reshape(TM, 4, part, 128)
    w_all = jnp.transpose(held[:, :3], (0, 2, 1, 3)).reshape(width, 384)
    w_out_t = held[:, 3].reshape(width, 128)

    wide = frames.astype(F32)
    mean_square = jnp.mean(wide * wide, axis=-1, keepdims=True)
    normed = (wide * lax.rsqrt(mean_square + 1e-06) * norm_gain).astype(BF16)
    projected = jnp.dot(normed, w_all, preferred_element_type=F32).astype(BF16)
    query, kv = projected[:, :128], projected[:, 128:]

    slope = slopes[0] * LOG2E
    spot = jnp.arange(rows, dtype=jnp.int32)
    ahead = (spot[None, :] - spot[:, None]).astype(F32) * slope
    apart = jnp.abs(ahead)
    bias = jnp.stack([-ahead, ahead, -apart, apart])
    moves = [0]
    for step in range(1, Z // 2):
        moves += [step, -step]
    moves.append(Z // 2)
    key_block = (yh * Z + (z + jnp.array(moves, jnp.int32)) % Z) * CORE + core
    turn = jnp.arange(4, dtype=jnp.int32)
    query_block = ((yh + turn % 2) % 2 * Z + z) * CORE + (core + turn // 2) % 2
    gap = (key_block[:, None] - query_block[None, :]) % TM
    half = TM // 2
    kinds = jnp.where(gap == 0, 2, jnp.where(gap < half, 0, jnp.where(gap == half, 3, 1)))
    bases = jnp.minimum(gap, TM - gap).astype(F32) * rows * slope
    kinds, bases = kinds.astype(jnp.int32).reshape(-1), bases.reshape(-1)

    both = jnp.concatenate([query, tm_permute(query, 1, 0, 0)], axis=0)
    queries = jnp.concatenate([both, tm_permute(both, 0, 0, 1)], axis=0)

    scale = 128 ** (-0.5) * LOG2E
    step_of = functools.partial(attention_step, kinds, bases, queries)
    up = tm_permute(kv, 0, 1, 0)
    down = tm_permute(kv, 0, -1, 0)
    state = step_of([kv], bias, None, 0, False, scale)
    for step in range(1, Z // 2):
        next_up = tm_permute(up, 0, 1, 0)
        if step + 1 < Z // 2:
            next_down = tm_permute(down, 0, -1, 0)
        state = step_of([up, down], bias, state, 2 * step - 1, False, scale)
        up, down = next_up, next_down
    packed, out, lse = step_of([up], bias, state, Z - 1, True, scale)

    got = tm_permute(packed[2 * rows :], 0, 0, 1)
    send, keep, keep_lse = merge_core(out, lse, got, rows)
    got = tm_permute(send, 1, 0, 0)
    partial = merge_project(keep, keep_lse, got, w_out_t)
    heads = lax.axis_size("head")
    pieces = lax.all_to_all(
        partial.reshape(heads, rows // heads, width), "head", split_axis=0, concat_axis=0, tiled=True
    )
    return jnp.sum(pieces.astype(F32), axis=0).astype(BF16)


def solution(mesh):
    in_specs = (P("tm", None), P(), P(None, "tm", "head"), P("head"), P("head", "tm"))
    out_specs = P(("tm", "head"), None)
    return jax.shard_map(local, mesh=mesh, in_specs=in_specs, out_specs=out_specs, check_vma=False)
```

```python
import functools
import math

import jax
import jax.numpy as jnp
from jax import lax
from jax.experimental import pallas as pl
from jax.experimental.pallas import tpu as pltpu
from jax.sharding import PartitionSpec as P

F32, BF16 = jnp.float32, jnp.bfloat16
LOG2E = math.log2(math.e)
YH, Z, CORE = 2, 8, 2
TM = YH * Z * CORE


def tm_permute(x, d_yh, d_z, d_core):
    pairs = []
    for yh in range(YH):
        for z in range(Z):
            for core in range(CORE):
                source = ((yh + d_yh) % YH * Z + (z + d_z) % Z) * CORE + (core + d_core) % CORE
                pairs.append((source, (yh * Z + z) * CORE + core))
    return lax.ppermute(x, "tm", pairs)


def ring_permute(x):
    pairs = []
    for yh in range(YH):
        for z in range(Z):
            for core in range(CORE):
                ahead = 1 if core == 0 else -1
                pairs.append(((yh * Z + (z + ahead) % Z) * CORE + core, (yh * Z + z) * CORE + core))
    return lax.ppermute(x, "tm", pairs)


def project_kernel(mine_ref, other_ref, w_ref, query_ref, kv_ref):
    block = pl.program_id(0)

    def project(ref):
        query_ref[...] = jnp.dot(ref[...], w_ref[:, :128], preferred_element_type=F32).astype(BF16)

        @pl.when(block % 2 == 0)
        def _():
            kv_ref[...] = jnp.dot(ref[...], w_ref[:, 128:], preferred_element_type=F32).astype(BF16)

    @pl.when(block < 2)
    def _():
        project(mine_ref)

    @pl.when(block >= 2)
    def _():
        project(other_ref)


def project(mine, other, w_all, rows):
    width = mine.shape[1]
    return pl.pallas_call(
        project_kernel,
        out_shape=[jax.ShapeDtypeStruct((4 * rows, 128), BF16), jax.ShapeDtypeStruct((2 * rows, 256), BF16)],
        grid=(4,),
        in_specs=[
            pl.BlockSpec((rows, width), lambda i: (jnp.minimum(i, 1), 0)),
            pl.BlockSpec((rows, width), lambda i: (jnp.maximum(i - 2, 0), 0)),
            pl.BlockSpec((width, 384), lambda i: (0, 0)),
        ],
        out_specs=[
            pl.BlockSpec((rows, 128), lambda i: (i, 0)),
            pl.BlockSpec((rows, 256), lambda i: (i // 2, 0)),
        ],
    )(mine, other, w_all)


def split_bf16(x):
    high = x.astype(BF16)
    rest = x - high.astype(F32)
    mid = rest.astype(BF16)
    return high, mid, (rest - mid.astype(F32)).astype(BF16)


def pack_partial(out, lse):
    high, mid, low = split_bf16(lse)
    lane = lax.broadcasted_iota(jnp.int32, lse.shape, 1)
    stat = jnp.where(lane < 32, high.astype(F32), jnp.where(lane < 64, mid.astype(F32), low.astype(F32)))
    return jnp.concatenate([out.astype(BF16), stat.astype(BF16)], axis=1)


def unpack_partial(packed):
    out = packed[:, :128].astype(F32)
    stat = packed[:, 128:].astype(F32)
    lse = stat[:, 0:1] + stat[:, 32:33] + stat[:, 64:65]
    return out, jnp.broadcast_to(lse, out.shape)


def attention_kernel(shards, offset, first, last, scale, *refs):
    kind_ref, base_ref = refs[:2]
    q_ref = refs[2]
    kv_refs = refs[3 : 3 + shards]
    bias_refs = refs[3 + shards : 3 + 2 * shards]
    rest = refs[3 + 2 * shards :]
    if not first:
        peak_ref, sums_ref = rest[:2]
        rest = rest[2:]
    out_refs = rest
    block = pl.program_id(0)
    rows = q_ref.shape[0]
    keys = kv_refs[0].shape[0]
    chunk = 256
    ones = jnp.ones((keys, 128), BF16)
    bases = [base_ref[offset + 4 * j + block] for j in range(shards)]
    for start in range(0, rows, chunk):
        here = pl.ds(start, chunk)
        query = q_ref[here, :]
        scores, top = [], None
        for j in range(shards):
            score = lax.dot_general(
                query, kv_refs[j][:, :128], (((1,), (1,)), ((), ())), preferred_element_type=F32
            )
            score = score * scale + bias_refs[j][0, here, :]
            scores.append(score)
            here_top = jnp.max(score, axis=1, keepdims=True) - bases[j]
            top = here_top if top is None else jnp.maximum(top, here_top)
        peak = jnp.broadcast_to(top, (chunk, 128))
        if not first:
            old = peak_ref[here, :]
            peak = jnp.maximum(peak, old)
        total = None
        for j in range(shards):
            weight = jnp.exp2(scores[j] - jnp.tile(peak + bases[j], (1, keys // 128))).astype(BF16)
            value = jnp.concatenate([kv_refs[j][:, 128:], ones], axis=1)
            part = jnp.dot(weight, value, preferred_element_type=F32)
            total = part if total is None else total + part
        if not first:
            total = total + sums_ref[here, :] * jnp.tile(jnp.exp2(old - peak), (1, 2))
        if last:
            norm = total[:, :128] / total[:, 128:]
            lse = peak + jnp.log2(total[:, 128:])

            @pl.when(block < 2)
            def _(norm=norm, lse=lse, here=here):
                out_refs[1][here, :] = norm
                out_refs[2][here, :] = lse

            @pl.when(block >= 2)
            def _(norm=norm, lse=lse, here=here):
                out_refs[0][here, :] = pack_partial(norm, lse)
        else:
            out_refs[0][here, :] = peak
            out_refs[1][here, :] = total


def attention_step(kinds, bases, query, bias, kv, shards, state, first_shard, last, scale):
    total_rows = query.shape[0]
    rows = keys = bias.shape[1]
    first = state is None
    offset = 4 * first_shard
    in_specs = [pl.BlockSpec((rows, 128), lambda i, kind, base: (i, 0))]
    in_specs += [pl.BlockSpec((keys, 256), lambda i, kind, base, j=j: (j, 0)) for j in range(shards)]
    for j in range(shards):
        in_specs.append(
            pl.BlockSpec((1, rows, keys), lambda i, kind, base, j=j: (kind[offset + 4 * j + i], 0, 0))
        )
    args = [kinds, bases, query] + [kv] * shards + [bias] * shards
    if not first:
        in_specs += [
            pl.BlockSpec((rows, 128), lambda i, kind, base: (i, 0)),
            pl.BlockSpec((rows, 256), lambda i, kind, base: (i, 0)),
        ]
        args += list(state)
    if last:
        half = total_rows // 2
        shapes = [((half, 256), BF16), ((half, 128), F32), ((half, 128), F32)]
        late = lambda i, kind, base: (jnp.maximum(i - 2, 0), 0)
        early = lambda i, kind, base: (jnp.minimum(i, 1), 0)
        where = [late, early, early]
    else:
        shapes = [((total_rows, 128), F32), ((total_rows, 256), F32)]
        where = [lambda i, kind, base: (i, 0)] * 2
    out_specs = [pl.BlockSpec((rows, s[1]), index) for (s, _), index in zip(shapes, where)]
    return pl.pallas_call(
        functools.partial(attention_kernel, shards, offset, first, last, scale),
        out_shape=[jax.ShapeDtypeStruct(s, t) for s, t in shapes],
        grid_spec=pltpu.PrefetchScalarGridSpec(
            num_scalar_prefetch=2,
            grid=(total_rows // rows,),
            in_specs=in_specs,
            out_specs=out_specs,
        ),
        cost_estimate=pl.CostEstimate(
            flops=4 * total_rows * keys * shards * 256,
            bytes_accessed=total_rows * 3072 + shards * keys * 512,
            transcendentals=total_rows * keys * shards,
        ),
    )(*args)


def merge(out_a, lse_a, out_b, lse_b):
    top = jnp.maximum(lse_a, lse_b)
    part_a, part_b = jnp.exp2(lse_a - top), jnp.exp2(lse_b - top)
    both = part_a + part_b
    return (out_a * part_a + out_b * part_b) / both, top + jnp.log2(both)


def merge_core_kernel(out_ref, lse_ref, got_ref, send_ref, keep_ref, keep_lse_ref):
    block = pl.program_id(0)
    got, got_lse = unpack_partial(got_ref[...])
    out, lse = merge(out_ref[...], lse_ref[...], got, got_lse)

    @pl.when(block == 0)
    def _():
        keep_ref[...] = out
        keep_lse_ref[...] = lse

    @pl.when(block == 1)
    def _():
        send_ref[...] = pack_partial(out, lse)


def merge_core(out, lse, got, rows):
    row_block = lambda i: (i, 0)
    fixed = lambda i: (0, 0)
    return pl.pallas_call(
        merge_core_kernel,
        out_shape=[
            jax.ShapeDtypeStruct((rows, 256), BF16),
            jax.ShapeDtypeStruct((rows, 128), F32),
            jax.ShapeDtypeStruct((rows, 128), F32),
        ],
        grid=(2,),
        in_specs=[
            pl.BlockSpec((rows, 128), row_block),
            pl.BlockSpec((rows, 128), row_block),
            pl.BlockSpec((rows, 256), row_block),
        ],
        out_specs=[
            pl.BlockSpec((rows, 256), fixed),
            pl.BlockSpec((rows, 128), fixed),
            pl.BlockSpec((rows, 128), fixed),
        ],
    )(out, lse, got)


def merge_project_kernel(out_ref, lse_ref, got_ref, w_ref, partial_ref):
    got, got_lse = unpack_partial(got_ref[...])
    out, _ = merge(out_ref[...], lse_ref[...], got, got_lse)
    partial_ref[...] = lax.dot_general(
        out.astype(BF16), w_ref[...], (((1,), (1,)), ((), ())), preferred_element_type=F32
    ).astype(BF16)


def merge_project(out, lse, got, w_out_t):
    rows, width = out.shape[0], w_out_t.shape[0]
    return pl.pallas_call(
        merge_project_kernel,
        out_shape=jax.ShapeDtypeStruct((rows, width), BF16),
    )(out, lse, got, w_out_t)


def local(frames, norm_gain, w_qkv, slopes, w_out):
    rows, width = frames.shape
    me = lax.axis_index("tm")
    core, z, yh = me % CORE, me // CORE % Z, me // (CORE * Z)

    wide = frames.astype(F32)
    mean_square = jnp.mean(wide * wide, axis=-1, keepdims=True)
    normed = (wide * lax.rsqrt(mean_square + 1e-06) * norm_gain).astype(BF16)
    mine = jnp.concatenate([normed, tm_permute(normed, 1, 0, 0)], axis=0)
    other = tm_permute(mine, 0, 0, 1)

    slope = slopes[0] * LOG2E
    spot = jnp.arange(rows, dtype=jnp.int32)
    rise = (spot[None, :] - spot[:, None]).astype(F32) * slope
    apart = jnp.abs(rise)
    bias = jnp.stack([-rise, rise, -apart, apart])
    ahead = 1 - 2 * core
    far = jnp.array([0, 1, 1, 2, 2, 3, 3, 4], jnp.int32)
    flip = jnp.array([0, 0, 1, 0, 1, 0, 1, 0], jnp.int32)
    key_block = (yh * Z + (z + ahead * far) % Z) * CORE + (core + flip) % 2
    turn = jnp.arange(4, dtype=jnp.int32)
    query_block = ((yh + turn % 2) % 2 * Z + z) * CORE + (core + turn // 2) % 2
    gap = (key_block[:, None] - query_block[None, :]) % TM
    half = TM // 2
    kinds = jnp.where(gap == 0, 2, jnp.where(gap < half, 0, jnp.where(gap == half, 3, 1)))
    bases = jnp.minimum(gap, TM - gap).astype(F32) * rows * slope
    kinds, bases = kinds.astype(jnp.int32).reshape(-1), bases.reshape(-1)

    part = w_qkv.shape[1]
    own = jnp.concatenate([w_qkv.reshape(3 * part, 128), w_out.T], axis=0)
    held = jnp.zeros((Z,) + own.shape, BF16)
    held = lax.dynamic_update_slice(held, own[None], (z, 0, 0))
    up = down = own
    for step in range(1, Z // 2 + 1):
        up = tm_permute(up, 0, 1, 0)
        held = lax.dynamic_update_slice(held, up[None], ((z + step) % Z, 0, 0))
        if step < Z // 2:
            down = tm_permute(down, 0, -1, 0)
            held = lax.dynamic_update_slice(held, down[None], ((z - step) % Z, 0, 0))
    held, bias, kinds, bases = lax.optimization_barrier((held, bias, kinds, bases))
    far = tm_permute(held, 1, 0, 0)
    flip = yh == 1
    held = jnp.stack([jnp.where(flip, far, held), jnp.where(flip, held, far)])
    far = tm_permute(held, 0, 0, 1)
    flip = core == 1
    held = jnp.stack([jnp.where(flip, far, held), jnp.where(flip, held, far)], axis=2)
    held = held.reshape(TM, 4, part, 128)
    w_all = jnp.transpose(held[:, :3], (0, 2, 1, 3)).reshape(width, 384)
    w_out_t = held[:, 3].reshape(width, 128)

    queries, kv = project(mine, other, w_all, rows)

    scale = 128 ** (-0.5) * LOG2E
    step_of = functools.partial(attention_step, kinds, bases, queries, bias)
    coming = ring_permute(kv)
    state = step_of(kv, 1, None, 0, False, scale)
    for step in range(1, Z // 2):
        held = coming
        coming = ring_permute(held if step < Z // 2 - 1 else held[:rows])
        state = step_of(held, 2, state, 2 * step - 1, False, scale)
    packed, out, lse = step_of(coming, 1, state, Z - 1, True, scale)

    got = tm_permute(packed, 0, 0, 1)
    send, keep, keep_lse = merge_core(out, lse, got, rows)
    got = tm_permute(send, 1, 0, 0)
    partial = merge_project(keep, keep_lse, got, w_out_t)
    heads = lax.axis_size("head")
    pieces = lax.all_to_all(
        partial.reshape(heads, rows // heads, width), "head", split_axis=0, concat_axis=0, tiled=True
    )
    return jnp.sum(pieces.astype(F32), axis=0).astype(BF16)


def solution(mesh):
    in_specs = (P("tm", None), P(), P(None, "tm", "head"), P("head"), P("head", "tm"))
    out_specs = P(("tm", "head"), None)
    return jax.shard_map(local, mesh=mesh, in_specs=in_specs, out_specs=out_specs, check_vma=False)
```

```python
import functools
import math

import jax
import jax.numpy as jnp
from jax import lax
from jax.experimental import pallas as pl
from jax.experimental.pallas import tpu as pltpu
from jax.sharding import PartitionSpec as P

F32, BF16 = jnp.float32, jnp.bfloat16
LOG2E = math.log2(math.e)
YH, Z, CORE = 2, 8, 2
TM = YH * Z * CORE


def tm_permute(x, d_yh, d_z, d_core):
    pairs = []
    for yh in range(YH):
        for z in range(Z):
            for core in range(CORE):
                source = ((yh + d_yh) % YH * Z + (z + d_z) % Z) * CORE + (core + d_core) % CORE
                pairs.append((source, (yh * Z + z) * CORE + core))
    return lax.ppermute(x, "tm", pairs)


def split_bf16(x):
    high = x.astype(BF16)
    rest = x - high.astype(F32)
    mid = rest.astype(BF16)
    return high, mid, (rest - mid.astype(F32)).astype(BF16)


def pack_partial(out, lse):
    high, mid, low = split_bf16(lse)
    lane = lax.broadcasted_iota(jnp.int32, lse.shape, 1)
    stat = jnp.where(lane < 32, high.astype(F32), jnp.where(lane < 64, mid.astype(F32), low.astype(F32)))
    return jnp.concatenate([out.astype(BF16), stat.astype(BF16)], axis=1)


def unpack_partial(packed):
    out = packed[:, :128].astype(F32)
    stat = packed[:, 128:].astype(F32)
    lse = stat[:, 0:1] + stat[:, 32:33] + stat[:, 64:65]
    return out, jnp.broadcast_to(lse, out.shape)


def attention_kernel(shards, scale, blocks, *refs):
    sign_ref, base_ref, slope_ref, query_ref = refs[:4]
    kv_refs = refs[4 : 4 + shards]
    send_ref, keep_ref, keep_lse_ref = refs[4 + shards :]
    step = pl.program_id(0)
    rows = query_ref.shape[0]
    keys = kv_refs[0].shape[0]
    parts = keys // rows
    block = step // parts
    first_row = (step % parts) * rows
    query = query_ref[...]
    ones = jnp.ones((keys, 128), BF16)
    row = (lax.broadcasted_iota(jnp.int32, (rows, 128), 0) + first_row).astype(F32)
    column = lax.broadcasted_iota(jnp.int32, (1, keys), 1).astype(F32)
    peak = total = None
    for start in range(0, shards, 2):
        scores, offsets, top = [], [], None
        for j in (start, start + 1):
            sign, base = sign_ref[blocks * j + block], base_ref[blocks * j + block]
            score = lax.dot_general(
                query, kv_refs[j][:, :128], (((1,), (1,)), ((), ())), preferred_element_type=F32
            )
            if j == 0:
                slope = jnp.where(block == 0, -slope_ref[0], slope_ref[0])
                score = score * scale + jnp.abs(column - row[:, :1]) * slope
                offset = jnp.full((rows, 128), base, F32)
            else:
                score = score * scale + column * sign
                offset = row * sign + base
            scores.append(score)
            offsets.append(offset)
            here_top = jnp.broadcast_to(jnp.max(score, axis=1, keepdims=True), (rows, 128)) - offset
            top = here_top if top is None else jnp.maximum(top, here_top)
        old = peak
        peak = top if old is None else jnp.maximum(top, old)
        part = None
        for j, score, offset in zip((start, start + 1), scores, offsets):
            weight = jnp.exp2(score - jnp.tile(peak + offset, (1, keys // 128))).astype(BF16)
            value = jnp.concatenate([kv_refs[j][:, 128:], ones], axis=1)
            more = jnp.dot(weight, value, preferred_element_type=F32)
            part = more if part is None else part + more
        total = part if total is None else part + total * jnp.tile(jnp.exp2(old - peak), (1, 2))
    out = total[:, :128] / total[:, 128:]
    lse = peak + jnp.log2(total[:, 128:])

    @pl.when(block == 0)
    def _():
        keep_ref[...] = out
        keep_lse_ref[...] = lse

    @pl.when(block == 1)
    def _():
        send_ref[...] = pack_partial(out, lse)


def attention(signs, bases, slope, query, kvs, scale):
    blocks, shards = 2, len(kvs)
    keys = kvs[0].shape[0]
    rows = keys // 2
    early = lambda i, *_: (jnp.minimum(i, 1), 0)
    late = lambda i, *_: (jnp.maximum(i - 2, 0), 0)
    return pl.pallas_call(
        functools.partial(attention_kernel, shards, scale, blocks),
        out_shape=[
            jax.ShapeDtypeStruct((keys, 256), BF16),
            jax.ShapeDtypeStruct((keys, 128), F32),
            jax.ShapeDtypeStruct((keys, 128), F32),
        ],
        grid_spec=pltpu.PrefetchScalarGridSpec(
            num_scalar_prefetch=3,
            grid=(blocks * 2,),
            in_specs=[pl.BlockSpec((rows, 128), lambda i, *_: (i, 0))]
            + [pl.BlockSpec((keys, 256), lambda i, *_: (0, 0)) for _ in kvs],
            out_specs=[
                pl.BlockSpec((rows, 256), late),
                pl.BlockSpec((rows, 128), early),
                pl.BlockSpec((rows, 128), early),
            ],
        ),
        cost_estimate=pl.CostEstimate(
            flops=4 * blocks * keys * keys * shards * 256,
            bytes_accessed=shards * keys * 512 + blocks * keys * 1024,
            transcendentals=blocks * keys * keys * shards,
        ),
    )(signs, bases, slope, query, *kvs)


def merge(out_a, lse_a, out_b, lse_b):
    top = jnp.maximum(lse_a, lse_b)
    part_a, part_b = jnp.exp2(lse_a - top), jnp.exp2(lse_b - top)
    both = part_a + part_b
    return (out_a * part_a + out_b * part_b) / both, top + jnp.log2(both)


def merge_project_kernel(out_ref, lse_ref, got_ref, w_ref, partial_ref):
    got, got_lse = unpack_partial(got_ref[...])
    out, _ = merge(out_ref[...], lse_ref[...], got, got_lse)
    partial_ref[...] = lax.dot_general(
        out.astype(BF16), w_ref[...], (((1,), (1,)), ((), ())), preferred_element_type=F32
    ).astype(BF16)


def merge_project(out, lse, got, w_out_t):
    rows, width = out.shape[0], w_out_t.shape[0]
    return pl.pallas_call(
        merge_project_kernel,
        out_shape=jax.ShapeDtypeStruct((rows, width), BF16),
    )(out, lse, got, w_out_t)


def local(frames, norm_gain, w_qkv, slopes, w_out):
    rows, width = frames.shape
    me = lax.axis_index("tm")
    core, z, yh = me % CORE, me // CORE % Z, me // (CORE * Z)

    part = w_qkv.shape[1]
    own = jnp.concatenate([w_qkv.reshape(3 * part, 128), w_out.T], axis=0)
    held = jnp.zeros((Z,) + own.shape, BF16)
    held = lax.dynamic_update_slice(held, own[None], (z, 0, 0))
    up = down = own
    for step in range(1, Z // 2 + 1):
        up = tm_permute(up, 0, 1, 0)
        held = lax.dynamic_update_slice(held, up[None], ((z + step) % Z, 0, 0))
        if step < Z // 2:
            down = tm_permute(down, 0, -1, 0)
            held = lax.dynamic_update_slice(held, down[None], ((z - step) % Z, 0, 0))
    other = tm_permute(held, 1, 0, 0)
    flip = yh == 1
    held = jnp.stack([jnp.where(flip, other, held), jnp.where(flip, held, other)])
    other = tm_permute(held, 0, 0, 1)
    flip = core == 1
    held = jnp.stack([jnp.where(flip, other, held), jnp.where(flip, held, other)], axis=2)
    held = held.reshape(TM, 4, part, 128)
    w_all = jnp.transpose(held[:, :3], (0, 2, 1, 3)).reshape(width, 384)
    w_out_t = held[:, 3].reshape(width, 128)

    wide = frames.astype(F32)
    mean_square = jnp.mean(wide * wide, axis=-1, keepdims=True)
    normed = (wide * lax.rsqrt(mean_square + 1e-06) * norm_gain).astype(BF16)
    projected = jnp.dot(normed, w_all, preferred_element_type=F32).astype(BF16)
    query, kv = projected[:, :128], projected[:, 128:]

    slope = slopes * LOG2E
    ring = [0]
    for step in range(1, Z // 2):
        ring += [step, -step]
    ring.append(Z // 2)
    far = jnp.array([move for move in ring for _ in range(CORE)], jnp.int32)
    swap = jnp.array([0, 1] * Z, jnp.int32)
    key_block = (yh * Z + (z + far) % Z) * CORE + (core + swap) % CORE
    query_block = ((yh + jnp.arange(YH, dtype=jnp.int32)) % YH * Z + z) * CORE + core
    gap = (key_block[:, None] - query_block[None, :]) % TM
    signs = jnp.where(gap < TM // 2, -slope[0], slope[0]).reshape(-1)
    bases = (jnp.minimum(gap, TM - gap).astype(F32) * (rows * slope[0])).reshape(-1)

    up = tm_permute(kv, 0, 1, 0)
    down = tm_permute(kv, 0, -1, 0)
    kvs = [kv, tm_permute(kv, 0, 0, 1)]
    queries = jnp.concatenate([query, tm_permute(query, 1, 0, 0)], axis=0)
    for step in range(1, Z // 2 + 1):
        got = [up] if step == Z // 2 else [up, down]
        if step < Z // 2:
            up = tm_permute(up, 0, 1, 0)
        if step < Z // 2 - 1:
            down = tm_permute(down, 0, -1, 0)
        for piece in got:
            kvs += [piece, tm_permute(piece, 0, 0, 1)]

    send, keep, keep_lse = attention(signs, bases, slope, queries, kvs, 128 ** (-0.5) * LOG2E)
    got = tm_permute(send, 1, 0, 0)
    partial = merge_project(keep, keep_lse, got, w_out_t)
    heads = lax.axis_size("head")
    pieces = lax.all_to_all(
        partial.reshape(heads, rows // heads, width), "head", split_axis=0, concat_axis=0, tiled=True
    )
    return jnp.sum(pieces.astype(F32), axis=0).astype(BF16)


def solution(mesh):
    in_specs = (P("tm", None), P(), P(None, "tm", "head"), P("head"), P("head", "tm"))
    out_specs = P(("tm", "head"), None)
    return jax.shard_map(local, mesh=mesh, in_specs=in_specs, out_specs=out_specs, check_vma=False)
```

```python
import functools
import math

import jax
import jax.numpy as jnp
from jax import lax
from jax.experimental import pallas as pl
from jax.experimental.pallas import tpu as pltpu
from jax.sharding import PartitionSpec as P

F32, BF16 = jnp.float32, jnp.bfloat16
LOG2E = math.log2(math.e)
YH, Z, CORE = 2, 8, 2
TM = YH * Z * CORE
YL, X = 2, 4


def tm_permute(x, d_yh, d_z, d_core):
    pairs = []
    for yh in range(YH):
        for z in range(Z):
            for core in range(CORE):
                source = ((yh + d_yh) % YH * Z + (z + d_z) % Z) * CORE + (core + d_core) % CORE
                pairs.append((source, (yh * Z + z) * CORE + core))
    return lax.ppermute(x, "tm", pairs)


def head_permute(x, d_yl, d_x):
    pairs = []
    for yl in range(YL):
        for column in range(X):
            pairs.append(((yl + d_yl) % YL * X + (column + d_x) % X, yl * X + column))
    return lax.ppermute(x, "head", pairs)


def split_bf16(x):
    high = x.astype(BF16)
    rest = x - high.astype(F32)
    mid = rest.astype(BF16)
    return high, mid, (rest - mid.astype(F32)).astype(BF16)


def pack_partial(out, lse):
    high, mid, low = split_bf16(lse)
    lane = lax.broadcasted_iota(jnp.int32, lse.shape, 1)
    stat = jnp.where(lane < 32, high.astype(F32), jnp.where(lane < 64, mid.astype(F32), low.astype(F32)))
    return jnp.concatenate([out.astype(BF16), stat.astype(BF16)], axis=1)


def unpack_partial(packed):
    out = packed[:, :128].astype(F32)
    stat = packed[:, 128:].astype(F32)
    lse = stat[:, 0:1] + stat[:, 32:33] + stat[:, 64:65]
    return out, jnp.broadcast_to(lse, out.shape)


def attention_kernel(shards, scale, blocks, *refs):
    sign_ref, base_ref, slope_ref, query_ref = refs[:4]
    kv_refs = refs[4 : 4 + shards]
    send_ref, keep_ref, keep_lse_ref = refs[4 + shards :]
    step = pl.program_id(0)
    rows = query_ref.shape[0]
    keys = kv_refs[0].shape[0]
    parts = keys // rows
    block = step // parts
    first_row = (step % parts) * rows
    query = query_ref[...]
    ones = jnp.ones((keys, 128), BF16)
    row = (lax.broadcasted_iota(jnp.int32, (rows, 128), 0) + first_row).astype(F32)
    column = lax.broadcasted_iota(jnp.int32, (1, keys), 1).astype(F32)
    peak = total = None
    for start in range(0, shards, 2):
        scores, offsets, top = [], [], None
        for j in (start, start + 1):
            sign, base = sign_ref[blocks * j + block], base_ref[blocks * j + block]
            score = lax.dot_general(
                query, kv_refs[j][:, :128], (((1,), (1,)), ((), ())), preferred_element_type=F32
            )
            if j == 0:
                slope = jnp.where(block == 0, -slope_ref[0], slope_ref[0])
                score = score * scale + jnp.abs(column - row[:, :1]) * slope
                offset = jnp.full((rows, 128), base, F32)
            else:
                score = score * scale + column * sign
                offset = row * sign + base
            scores.append(score)
            offsets.append(offset)
            here_top = jnp.broadcast_to(jnp.max(score, axis=1, keepdims=True), (rows, 128)) - offset
            top = here_top if top is None else jnp.maximum(top, here_top)
        old = peak
        peak = top if old is None else jnp.maximum(top, old)
        part = None
        for j, score, offset in zip((start, start + 1), scores, offsets):
            weight = jnp.exp2(score - jnp.tile(peak + offset, (1, keys // 128))).astype(BF16)
            value = jnp.concatenate([kv_refs[j][:, 128:], ones], axis=1)
            more = jnp.dot(weight, value, preferred_element_type=F32)
            part = more if part is None else part + more
        total = part if total is None else part + total * jnp.tile(jnp.exp2(old - peak), (1, 2))
    out = total[:, :128] / total[:, 128:]
    lse = peak + jnp.log2(total[:, 128:])

    @pl.when(block == 0)
    def _():
        keep_ref[...] = out
        keep_lse_ref[...] = lse

    @pl.when(block == 1)
    def _():
        send_ref[...] = pack_partial(out, lse)


def attention(signs, bases, slope, query, kvs, scale):
    blocks, shards = 2, len(kvs)
    keys = kvs[0].shape[0]
    rows = keys // 2
    early = lambda i, *_: (jnp.minimum(i, 1), 0)
    late = lambda i, *_: (jnp.maximum(i - 2, 0), 0)
    return pl.pallas_call(
        functools.partial(attention_kernel, shards, scale, blocks),
        out_shape=[
            jax.ShapeDtypeStruct((keys, 256), BF16),
            jax.ShapeDtypeStruct((keys, 128), F32),
            jax.ShapeDtypeStruct((keys, 128), F32),
        ],
        grid_spec=pltpu.PrefetchScalarGridSpec(
            num_scalar_prefetch=3,
            grid=(blocks * 2,),
            in_specs=[pl.BlockSpec((rows, 128), lambda i, *_: (i, 0))]
            + [pl.BlockSpec((keys, 256), lambda i, *_: (0, 0)) for _ in kvs],
            out_specs=[
                pl.BlockSpec((rows, 256), late),
                pl.BlockSpec((rows, 128), early),
                pl.BlockSpec((rows, 128), early),
            ],
        ),
        cost_estimate=pl.CostEstimate(
            flops=4 * blocks * keys * keys * shards * 256,
            bytes_accessed=shards * keys * 512 + blocks * keys * 1024,
            transcendentals=blocks * keys * keys * shards,
        ),
    )(signs, bases, slope, query, *kvs)


def merge(out_a, lse_a, out_b, lse_b):
    top = jnp.maximum(lse_a, lse_b)
    part_a, part_b = jnp.exp2(lse_a - top), jnp.exp2(lse_b - top)
    both = part_a + part_b
    return (out_a * part_a + out_b * part_b) / both, top + jnp.log2(both)


def merge_kernel(out_ref, lse_ref, got_ref, mixed_ref):
    got, got_lse = unpack_partial(got_ref[...])
    mixed_ref[...] = merge(out_ref[...], lse_ref[...], got, got_lse)[0].astype(BF16)


def merge_halves(out, lse, got):
    return pl.pallas_call(merge_kernel, out_shape=jax.ShapeDtypeStruct(out.shape, BF16))(out, lse, got)


def output_kernel(head_ref, mixed_ref, *refs):
    out_ref = refs[-1]
    total = None
    for j, weight_ref in enumerate(refs[:-1]):
        for turn in range(YL):
            part = lax.dot_general(
                mixed_ref[head_ref[YL * j + turn]],
                weight_ref[turn],
                (((1,), (1,)), ((), ())),
                preferred_element_type=F32,
            )
            total = part if total is None else total + part
    out_ref[...] = total.astype(BF16)


def output_projection(heads, mixed, weights):
    rows, width = mixed.shape[1], weights[0].shape[1]
    return pl.pallas_call(
        output_kernel,
        out_shape=jax.ShapeDtypeStruct((rows, width), BF16),
        grid_spec=pltpu.PrefetchScalarGridSpec(
            num_scalar_prefetch=1,
            grid=(1,),
            in_specs=[pl.BlockSpec(mixed.shape, lambda i, _: (0, 0, 0))]
            + [pl.BlockSpec(w.shape, lambda i, _: (0, 0, 0)) for w in weights],
            out_specs=pl.BlockSpec((rows, width), lambda i, _: (0, 0)),
        ),
    )(heads, mixed, *weights)


def local(frames, norm_gain, w_qkv, slopes, w_out):
    rows, width = frames.shape
    me = lax.axis_index("tm")
    core, z, yh = me % CORE, me // CORE % Z, me // (CORE * Z)

    part = w_qkv.shape[1]
    own = jnp.concatenate([w_qkv.reshape(3 * part, 128), w_out.T], axis=0)
    above, below = tm_permute(own, 0, 1, 0), tm_permute(own, 0, -1, 0)
    trio = jnp.stack([below, own, above])
    high = tm_permute(trio, 0, 3, 0)
    low = tm_permute(trio[1:], 0, -3, 0)
    held = jnp.zeros((Z,) + own.shape, BF16)
    found = [low[0], low[1], below, own, above, high[0], high[1], high[2]]
    for move, piece in zip(range(-3, 5), found):
        held = lax.dynamic_update_slice(held, piece[None], ((z + move) % Z, 0, 0))
    other = tm_permute(held, 1, 0, 0)
    flip = yh == 1
    held = jnp.stack([jnp.where(flip, other, held), jnp.where(flip, held, other)])
    other = tm_permute(held, 0, 0, 1)
    flip = core == 1
    held = jnp.stack([jnp.where(flip, other, held), jnp.where(flip, held, other)], axis=2)
    held = held.reshape(TM, 4, part, 128)
    w_all = jnp.transpose(held[:, :3], (0, 2, 1, 3)).reshape(width, 384)
    w_out_t = held[:, 3].reshape(width, 128)

    wide = frames.astype(F32)
    mean_square = jnp.mean(wide * wide, axis=-1, keepdims=True)
    normed = (wide * lax.rsqrt(mean_square + 1e-06) * norm_gain).astype(BF16)
    projected = jnp.dot(normed, w_all, preferred_element_type=F32).astype(BF16)
    query, kv = projected[:, :128], projected[:, 128:]

    slope = slopes * LOG2E
    ring = [0]
    for step in range(1, Z // 2):
        ring += [step, -step]
    ring.append(Z // 2)
    far = jnp.array([move for move in ring for _ in range(CORE)], jnp.int32)
    swap = jnp.array([0, 1] * Z, jnp.int32)
    key_block = (yh * Z + (z + far) % Z) * CORE + (core + swap) % CORE
    query_block = ((yh + jnp.arange(YH, dtype=jnp.int32)) % YH * Z + z) * CORE + core
    gap = (key_block[:, None] - query_block[None, :]) % TM
    signs = jnp.where(gap < TM // 2, -slope[0], slope[0]).reshape(-1)
    bases = (jnp.minimum(gap, TM - gap).astype(F32) * (rows * slope[0])).reshape(-1)

    up = tm_permute(kv, 0, 1, 0)
    down = tm_permute(kv, 0, -1, 0)
    kvs = [kv, tm_permute(kv, 0, 0, 1)]
    queries = jnp.concatenate([query, tm_permute(query, 1, 0, 0)], axis=0)
    for step in range(1, Z // 2 + 1):
        if step == 1:
            up, w_out_t = lax.optimization_barrier((up, w_out_t))
            weights = [jnp.stack([w_out_t, head_permute(w_out_t, 1, 0)])]
        elif step == 2:
            up, weights[0] = lax.optimization_barrier((up, weights[0]))
            weights += [head_permute(weights[0], 0, 1), head_permute(weights[0], 0, -1)]
        elif step == 4:
            up, weights[1] = lax.optimization_barrier((up, weights[1]))
            weights.append(head_permute(weights[1], 0, 1))
        got = [up] if step == Z // 2 else [up, down]
        if step < Z // 2:
            up = tm_permute(up, 0, 1, 0)
        if step < Z // 2 - 1:
            down = tm_permute(down, 0, -1, 0)
        for piece in got:
            kvs += [piece, tm_permute(piece, 0, 0, 1)]

    send, keep, keep_lse = attention(signs, bases, slope, queries, kvs, 128 ** (-0.5) * LOG2E)
    got = tm_permute(send, 1, 0, 0)
    mixed = merge_halves(keep, keep_lse, got).reshape(YL * X, rows // (YL * X), 128)
    mixed = lax.all_to_all(mixed, "head", split_axis=0, concat_axis=0, tiled=True)
    place = lax.axis_index("head")
    turn, shift = jnp.array([0, 1] * X, jnp.int32), jnp.array([0, 0, 1, 1, 3, 3, 2, 2], jnp.int32)
    heads = (place // X + turn) % YL * X + (place + shift) % X
    return output_projection(heads, mixed, weights)


def solution(mesh):
    in_specs = (P("tm", None), P(), P(None, "tm", "head"), P("head"), P("head", "tm"))
    out_specs = P(("tm", "head"), None)
    return jax.shard_map(local, mesh=mesh, in_specs=in_specs, out_specs=out_specs, check_vma=False)
```

```python
import functools
import math

import jax
import jax.numpy as jnp
from jax import lax
from jax.experimental import pallas as pl
from jax.experimental.pallas import tpu as pltpu
from jax.sharding import PartitionSpec as P

F32, BF16 = jnp.float32, jnp.bfloat16
LOG2E = math.log2(math.e)
YH, Z, CORE = 2, 8, 2
TM = YH * Z * CORE
YL, X = 2, 4


def tm_permute(x, d_yh, d_z, d_core):
    pairs = []
    for yh in range(YH):
        for z in range(Z):
            for core in range(CORE):
                source = ((yh + d_yh) % YH * Z + (z + d_z) % Z) * CORE + (core + d_core) % CORE
                pairs.append((source, (yh * Z + z) * CORE + core))
    return lax.ppermute(x, "tm", pairs)


def head_permute(x, d_yl, d_x):
    pairs = []
    for yl in range(YL):
        for column in range(X):
            pairs.append(((yl + d_yl) % YL * X + (column + d_x) % X, yl * X + column))
    return lax.ppermute(x, "head", pairs)


def split_bf16(x):
    high = x.astype(BF16)
    rest = x - high.astype(F32)
    mid = rest.astype(BF16)
    return high, mid, (rest - mid.astype(F32)).astype(BF16)


def pack_partial(out, lse):
    high, mid, low = split_bf16(lse)
    lane = lax.broadcasted_iota(jnp.int32, lse.shape, 1)
    stat = jnp.where(lane < 32, high.astype(F32), jnp.where(lane < 64, mid.astype(F32), low.astype(F32)))
    return jnp.concatenate([out.astype(BF16), stat.astype(BF16)], axis=1)


def unpack_partial(packed):
    out = packed[:, :128].astype(F32)
    stat = packed[:, 128:].astype(F32)
    lse = stat[:, 0:1] + stat[:, 32:33] + stat[:, 64:65]
    return out, jnp.broadcast_to(lse, out.shape)


def attention_kernel(shards, scale, blocks, *refs):
    sign_ref, base_ref, slope_ref, query_ref = refs[:4]
    kv_refs = refs[4 : 4 + shards]
    send_ref, keep_ref, keep_lse_ref = refs[4 + shards :]
    step = pl.program_id(0)
    rows = query_ref.shape[0]
    keys = kv_refs[0].shape[0]
    parts = keys // rows
    block = step // parts
    first_row = (step % parts) * rows
    query = query_ref[...]
    ones = jnp.ones((keys, 128), BF16)
    row = (lax.broadcasted_iota(jnp.int32, (rows, 128), 0) + first_row).astype(F32)
    column = lax.broadcasted_iota(jnp.int32, (1, keys), 1).astype(F32)
    peak = total = None
    for start in range(0, shards, 2):
        scores, offsets, top = [], [], None
        for j in (start, start + 1):
            sign, base = sign_ref[blocks * j + block], base_ref[blocks * j + block]
            score = lax.dot_general(
                query, kv_refs[j][:, :128], (((1,), (1,)), ((), ())), preferred_element_type=F32
            )
            if j == 0:
                slope = jnp.where(block == 0, -slope_ref[0], slope_ref[0])
                score = score * scale + jnp.abs(column - row[:, :1]) * slope
                offset = jnp.full((rows, 128), base, F32)
            else:
                score = score * scale + column * sign
                offset = row * sign + base
            scores.append(score)
            offsets.append(offset)
            here_top = jnp.broadcast_to(jnp.max(score, axis=1, keepdims=True), (rows, 128)) - offset
            top = here_top if top is None else jnp.maximum(top, here_top)
        old = peak
        peak = top if old is None else jnp.maximum(top, old)
        part = None
        for j, score, offset in zip((start, start + 1), scores, offsets):
            weight = jnp.exp2(score - jnp.tile(peak + offset, (1, keys // 128))).astype(BF16)
            value = jnp.concatenate([kv_refs[j][:, 128:], ones], axis=1)
            more = jnp.dot(weight, value, preferred_element_type=F32)
            part = more if part is None else part + more
        total = part if total is None else part + total * jnp.tile(jnp.exp2(old - peak), (1, 2))
    out = total[:, :128] / total[:, 128:]
    lse = peak + jnp.log2(total[:, 128:])

    @pl.when(block == 0)
    def _():
        keep_ref[...] = out
        keep_lse_ref[...] = lse

    @pl.when(block == 1)
    def _():
        send_ref[...] = pack_partial(out, lse)


def attention(signs, bases, slope, query, kvs, scale):
    blocks, shards = 2, len(kvs)
    keys = kvs[0].shape[0]
    rows = keys // 2
    early = lambda i, *_: (jnp.minimum(i, 1), 0)
    late = lambda i, *_: (jnp.maximum(i - 2, 0), 0)
    return pl.pallas_call(
        functools.partial(attention_kernel, shards, scale, blocks),
        out_shape=[
            jax.ShapeDtypeStruct((keys, 256), BF16),
            jax.ShapeDtypeStruct((keys, 128), F32),
            jax.ShapeDtypeStruct((keys, 128), F32),
        ],
        grid_spec=pltpu.PrefetchScalarGridSpec(
            num_scalar_prefetch=3,
            grid=(blocks * 2,),
            in_specs=[pl.BlockSpec((rows, 128), lambda i, *_: (i, 0))]
            + [pl.BlockSpec((keys, 256), lambda i, *_: (0, 0)) for _ in kvs],
            out_specs=[
                pl.BlockSpec((rows, 256), late),
                pl.BlockSpec((rows, 128), early),
                pl.BlockSpec((rows, 128), early),
            ],
        ),
        cost_estimate=pl.CostEstimate(
            flops=4 * blocks * keys * keys * shards * 256,
            bytes_accessed=shards * keys * 512 + blocks * keys * 1024,
            transcendentals=blocks * keys * keys * shards,
        ),
    )(signs, bases, slope, query, *kvs)


def merge(out_a, lse_a, out_b, lse_b):
    top = jnp.maximum(lse_a, lse_b)
    part_a, part_b = jnp.exp2(lse_a - top), jnp.exp2(lse_b - top)
    both = part_a + part_b
    return (out_a * part_a + out_b * part_b) / both, top + jnp.log2(both)


def merge_kernel(out_ref, lse_ref, got_ref, mixed_ref):
    got, got_lse = unpack_partial(got_ref[...])
    mixed_ref[...] = merge(out_ref[...], lse_ref[...], got, got_lse)[0].astype(BF16)


def merge_halves(out, lse, got):
    return pl.pallas_call(merge_kernel, out_shape=jax.ShapeDtypeStruct(out.shape, BF16))(out, lse, got)


def output_kernel(head_ref, mixed_ref, *refs):
    out_ref = refs[-1]
    total = None
    for j, weight_ref in enumerate(refs[:-1]):
        for turn in range(YL):
            part = lax.dot_general(
                mixed_ref[head_ref[YL * j + turn]],
                weight_ref[turn],
                (((1,), (1,)), ((), ())),
                preferred_element_type=F32,
            )
            total = part if total is None else total + part
    out_ref[...] = total.astype(BF16)


def output_projection(heads, mixed, weights):
    rows, width = mixed.shape[1], weights[0].shape[1]
    return pl.pallas_call(
        output_kernel,
        out_shape=jax.ShapeDtypeStruct((rows, width), BF16),
        grid_spec=pltpu.PrefetchScalarGridSpec(
            num_scalar_prefetch=1,
            grid=(1,),
            in_specs=[pl.BlockSpec(mixed.shape, lambda i, _: (0, 0, 0))]
            + [pl.BlockSpec(w.shape, lambda i, _: (0, 0, 0)) for w in weights],
            out_specs=pl.BlockSpec((rows, width), lambda i, _: (0, 0)),
        ),
    )(heads, mixed, *weights)


def local(frames, norm_gain, w_qkv, slopes, w_out):
    rows, width = frames.shape
    me = lax.axis_index("tm")
    core, z, yh = me % CORE, me // CORE % Z, me // (CORE * Z)

    part = w_qkv.shape[1]
    own = jnp.concatenate([w_qkv.reshape(3 * part, 128), w_out.T], axis=0)
    above, below = tm_permute(own, 0, 1, 0), tm_permute(own, 0, -1, 0)
    trio = jnp.stack([below, own, above])
    high = tm_permute(trio, 0, 3, 0)
    low = tm_permute(trio[1:], 0, -3, 0)
    held = jnp.zeros((Z,) + own.shape, BF16)
    found = [low[0], low[1], below, own, above, high[0], high[1], high[2]]
    for move, piece in zip(range(-3, 5), found):
        held = lax.dynamic_update_slice(held, piece[None], ((z + move) % Z, 0, 0))
    other = tm_permute(held, 1, 0, 0)
    flip = yh == 1
    held = jnp.stack([jnp.where(flip, other, held), jnp.where(flip, held, other)])
    other = tm_permute(held, 0, 0, 1)
    flip = core == 1
    held = jnp.stack([jnp.where(flip, other, held), jnp.where(flip, held, other)], axis=2)
    held = held.reshape(TM, 4, part, 128)
    w_all = jnp.transpose(held[:, :3], (0, 2, 1, 3)).reshape(width, 384)
    w_out_t = held[:, 3].reshape(width, 128)

    wide = frames.astype(F32)
    mean_square = jnp.mean(wide * wide, axis=-1, keepdims=True)
    normed = (wide * lax.rsqrt(mean_square + 1e-06) * norm_gain).astype(BF16)
    projected = jnp.dot(normed, w_all, preferred_element_type=F32).astype(BF16)
    query, kv = projected[:, :128], projected[:, 128:]

    slope = slopes * LOG2E
    ring = [0]
    for step in range(1, Z // 2):
        ring += [step, -step]
    ring.append(Z // 2)
    far = jnp.array([move for move in ring for _ in range(CORE)], jnp.int32)
    swap = jnp.array([0, 1] * Z, jnp.int32)
    key_block = (yh * Z + (z + far) % Z) * CORE + (core + swap) % CORE
    query_block = ((yh + jnp.arange(YH, dtype=jnp.int32)) % YH * Z + z) * CORE + core
    gap = (key_block[:, None] - query_block[None, :]) % TM
    signs = jnp.where(gap < TM // 2, -slope[0], slope[0]).reshape(-1)
    bases = (jnp.minimum(gap, TM - gap).astype(F32) * (rows * slope[0])).reshape(-1)

    up = tm_permute(kv, 0, 1, 0)
    down = tm_permute(kv, 0, -1, 0)
    kvs = [kv, tm_permute(kv, 0, 0, 1)]
    far_query = tm_permute(query, 1, 0, 0)
    for step in range(1, Z // 2 + 1):
        if step == 1:
            up, down, far_query, w_out_t = lax.optimization_barrier((up, down, far_query, w_out_t))
        elif step == 2:
            up, down, pair = lax.optimization_barrier((up, down, pair))
        elif step == 3:
            up, down = lax.optimization_barrier((up, down))
        else:
            up, east = lax.optimization_barrier((up, east))
        got = [up] if step == Z // 2 else [up, down]
        if step < Z // 2:
            up = tm_permute(up, 0, 1, 0)
        if step < Z // 2 - 1:
            down = tm_permute(down, 0, -1, 0)
        if step == 1:
            pair = jnp.stack([w_out_t, head_permute(w_out_t, 1, 0)])
        elif step == 2:
            east, west = head_permute(pair, 0, 1), head_permute(pair, 0, -1)
        elif step == Z // 2:
            weights = [pair, east, west, head_permute(east, 0, 1)]
        for piece in got:
            kvs += [piece, tm_permute(piece, 0, 0, 1)]
    queries = jnp.concatenate([query, far_query], axis=0)

    send, keep, keep_lse = attention(signs, bases, slope, queries, kvs, 128 ** (-0.5) * LOG2E)
    got = tm_permute(send, 1, 0, 0)
    mixed = merge_halves(keep, keep_lse, got).reshape(YL * X, rows // (YL * X), 128)
    mixed = lax.all_to_all(mixed, "head", split_axis=0, concat_axis=0, tiled=True)
    place = lax.axis_index("head")
    turn, shift = jnp.array([0, 1] * X, jnp.int32), jnp.array([0, 0, 1, 1, 3, 3, 2, 2], jnp.int32)
    heads = (place // X + turn) % YL * X + (place + shift) % X
    return output_projection(heads, mixed, weights)


def solution(mesh):
    in_specs = (P("tm", None), P(), P(None, "tm", "head"), P("head"), P("head", "tm"))
    out_specs = P(("tm", "head"), None)
    return jax.shard_map(local, mesh=mesh, in_specs=in_specs, out_specs=out_specs, check_vma=False)
```

```python
import functools
import math

import jax
import jax.numpy as jnp
from jax import lax
from jax.experimental import pallas as pl
from jax.experimental.pallas import tpu as pltpu
from jax.sharding import PartitionSpec as P

F32, BF16 = jnp.float32, jnp.bfloat16
LOG2E = math.log2(math.e)
YH, Z, CORE = 2, 8, 2
TM = YH * Z * CORE
YL, X = 2, 4


def tm_permute(x, d_yh, d_z, d_core):
    pairs = []
    for yh in range(YH):
        for z in range(Z):
            for core in range(CORE):
                source = ((yh + d_yh) % YH * Z + (z + d_z) % Z) * CORE + (core + d_core) % CORE
                pairs.append((source, (yh * Z + z) * CORE + core))
    return lax.ppermute(x, "tm", pairs)


def head_permute(x, d_yl, d_x):
    pairs = []
    for yl in range(YL):
        for column in range(X):
            pairs.append(((yl + d_yl) % YL * X + (column + d_x) % X, yl * X + column))
    return lax.ppermute(x, "head", pairs)


def split_bf16(x):
    high = x.astype(BF16)
    rest = x - high.astype(F32)
    mid = rest.astype(BF16)
    return high, mid, (rest - mid.astype(F32)).astype(BF16)


def pack_partial(out, lse):
    high, mid, low = split_bf16(lse)
    lane = lax.broadcasted_iota(jnp.int32, lse.shape, 1)
    stat = jnp.where(lane < 32, high.astype(F32), jnp.where(lane < 64, mid.astype(F32), low.astype(F32)))
    return jnp.concatenate([out.astype(BF16), stat.astype(BF16)], axis=1)


def unpack_partial(packed):
    out = packed[:, :128].astype(F32)
    stat = packed[:, 128:].astype(F32)
    lse = stat[:, 0:1] + stat[:, 32:33] + stat[:, 64:65]
    return out, jnp.broadcast_to(lse, out.shape)


def attention_kernel(shards, scale, blocks, *refs):
    sign_ref, base_ref, slope_ref, query_ref = refs[:4]
    kv_refs = refs[4 : 4 + shards]
    send_ref, keep_ref, keep_lse_ref = refs[4 + shards :]
    step = pl.program_id(0)
    rows = query_ref.shape[0]
    keys = kv_refs[0].shape[0]
    parts = keys // rows
    block = step // parts
    first_row = (step % parts) * rows
    query = query_ref[...]
    ones = jnp.ones((keys, 128), BF16)
    row = (lax.broadcasted_iota(jnp.int32, (rows, 128), 0) + first_row).astype(F32)
    column = lax.broadcasted_iota(jnp.int32, (1, keys), 1).astype(F32)
    peak = total = None
    for start in range(0, shards, 2):
        scores, offsets, top = [], [], None
        for j in (start, start + 1):
            sign, base = sign_ref[blocks * j + block], base_ref[blocks * j + block]
            score = lax.dot_general(
                query, kv_refs[j][:, :128], (((1,), (1,)), ((), ())), preferred_element_type=F32
            )
            if j == 0:
                slope = jnp.where(block == 0, -slope_ref[0], slope_ref[0])
                score = score * scale + jnp.abs(column - row[:, :1]) * slope
                offset = jnp.full((rows, 128), base, F32)
            else:
                score = score * scale + column * sign
                offset = row * sign + base
            scores.append(score)
            offsets.append(offset)
            here_top = jnp.broadcast_to(jnp.max(score, axis=1, keepdims=True), (rows, 128)) - offset
            top = here_top if top is None else jnp.maximum(top, here_top)
        old = peak
        peak = top if old is None else jnp.maximum(top, old)
        part = None
        for j, score, offset in zip((start, start + 1), scores, offsets):
            weight = jnp.exp2(score - jnp.tile(peak + offset, (1, keys // 128))).astype(BF16)
            value = jnp.concatenate([kv_refs[j][:, 128:], ones], axis=1)
            more = jnp.dot(weight, value, preferred_element_type=F32)
            part = more if part is None else part + more
        total = part if total is None else part + total * jnp.tile(jnp.exp2(old - peak), (1, 2))
    out = total[:, :128] / total[:, 128:]
    lse = peak + jnp.log2(total[:, 128:])

    @pl.when(block == 0)
    def _():
        keep_ref[...] = out
        keep_lse_ref[...] = lse

    @pl.when(block == 1)
    def _():
        send_ref[...] = pack_partial(out, lse)


def attention(signs, bases, slope, query, kvs, scale):
    blocks, shards = 2, len(kvs)
    keys = kvs[0].shape[0]
    rows = keys // 2
    early = lambda i, *_: (jnp.minimum(i, 1), 0)
    late = lambda i, *_: (jnp.maximum(i - 2, 0), 0)
    return pl.pallas_call(
        functools.partial(attention_kernel, shards, scale, blocks),
        out_shape=[
            jax.ShapeDtypeStruct((keys, 256), BF16),
            jax.ShapeDtypeStruct((keys, 128), F32),
            jax.ShapeDtypeStruct((keys, 128), F32),
        ],
        grid_spec=pltpu.PrefetchScalarGridSpec(
            num_scalar_prefetch=3,
            grid=(blocks * 2,),
            in_specs=[pl.BlockSpec((rows, 128), lambda i, *_: (i, 0))]
            + [pl.BlockSpec((keys, 256), lambda i, *_: (0, 0)) for _ in kvs],
            out_specs=[
                pl.BlockSpec((rows, 256), late),
                pl.BlockSpec((rows, 128), early),
                pl.BlockSpec((rows, 128), early),
            ],
        ),
        cost_estimate=pl.CostEstimate(
            flops=4 * blocks * keys * keys * shards * 256,
            bytes_accessed=shards * keys * 512 + blocks * keys * 1024,
            transcendentals=blocks * keys * keys * shards,
        ),
    )(signs, bases, slope, query, *kvs)


def merge(out_a, lse_a, out_b, lse_b):
    top = jnp.maximum(lse_a, lse_b)
    part_a, part_b = jnp.exp2(lse_a - top), jnp.exp2(lse_b - top)
    both = part_a + part_b
    return (out_a * part_a + out_b * part_b) / both, top + jnp.log2(both)


def merge_kernel(out_ref, lse_ref, got_ref, mixed_ref):
    got, got_lse = unpack_partial(got_ref[...])
    mixed_ref[...] = merge(out_ref[...], lse_ref[...], got, got_lse)[0].astype(BF16)


def merge_halves(out, lse, got):
    return pl.pallas_call(merge_kernel, out_shape=jax.ShapeDtypeStruct(out.shape, BF16))(out, lse, got)


def output_kernel(head_ref, mixed_ref, *refs):
    out_ref = refs[-1]
    total = None
    for j, weight_ref in enumerate(refs[:-1]):
        for turn in range(YL):
            part = lax.dot_general(
                mixed_ref[head_ref[YL * j + turn]],
                weight_ref[turn],
                (((1,), (1,)), ((), ())),
                preferred_element_type=F32,
            )
            total = part if total is None else total + part
    out_ref[...] = total.astype(BF16)


def output_projection(heads, mixed, weights):
    rows, width = mixed.shape[1], weights[0].shape[1]
    return pl.pallas_call(
        output_kernel,
        out_shape=jax.ShapeDtypeStruct((rows, width), BF16),
        grid_spec=pltpu.PrefetchScalarGridSpec(
            num_scalar_prefetch=1,
            grid=(1,),
            in_specs=[pl.BlockSpec(mixed.shape, lambda i, _: (0, 0, 0))]
            + [pl.BlockSpec(w.shape, lambda i, _: (0, 0, 0)) for w in weights],
            out_specs=pl.BlockSpec((rows, width), lambda i, _: (0, 0)),
        ),
    )(heads, mixed, *weights)


def local(frames, norm_gain, w_qkv, slopes, w_out):
    rows, width = frames.shape
    me = lax.axis_index("tm")
    core, z, yh = me % CORE, me // CORE % Z, me // (CORE * Z)

    part = w_qkv.shape[1]
    own = jnp.concatenate([w_qkv.reshape(3 * part, 128), w_out.T], axis=0)
    above, below = tm_permute(own, 0, 1, 0), tm_permute(own, 0, -1, 0)
    trio = jnp.stack([below, own, above])
    high = tm_permute(trio, 0, 3, 0)
    low = tm_permute(trio[1:], 0, -3, 0)
    held = jnp.zeros((Z,) + own.shape, BF16)
    found = [low[0], low[1], below, own, above, high[0], high[1], high[2]]
    for move, piece in zip(range(-3, 5), found):
        held = lax.dynamic_update_slice(held, piece[None], ((z + move) % Z, 0, 0))
    other = tm_permute(held, 1, 0, 0)
    flip = yh == 1
    held = jnp.stack([jnp.where(flip, other, held), jnp.where(flip, held, other)])
    other = tm_permute(held, 0, 0, 1)
    flip = core == 1
    held = jnp.stack([jnp.where(flip, other, held), jnp.where(flip, held, other)], axis=2)
    held = held.reshape(TM, 4, part, 128)
    w_all = jnp.transpose(held[:, :3], (0, 2, 1, 3)).reshape(width, 384)
    w_out_t = held[:, 3].reshape(width, 128)

    wide = frames.astype(F32)
    mean_square = jnp.mean(wide * wide, axis=-1, keepdims=True)
    normed = (wide * lax.rsqrt(mean_square + 1e-06) * norm_gain).astype(BF16)
    projected = jnp.dot(normed, w_all, preferred_element_type=F32).astype(BF16)
    query, kv = projected[:, :128], projected[:, 128:]

    slope = slopes * LOG2E
    ring = [0]
    for step in range(1, Z // 2):
        ring += [step, -step]
    ring.append(Z // 2)
    far = jnp.array([move for move in ring for _ in range(CORE)], jnp.int32)
    swap = jnp.array([0, 1] * Z, jnp.int32)
    key_block = (yh * Z + (z + far) % Z) * CORE + (core + swap) % CORE
    query_block = ((yh + jnp.arange(YH, dtype=jnp.int32)) % YH * Z + z) * CORE + core
    gap = (key_block[:, None] - query_block[None, :]) % TM
    signs = jnp.where(gap < TM // 2, -slope[0], slope[0]).reshape(-1)
    bases = (jnp.minimum(gap, TM - gap).astype(F32) * (rows * slope[0])).reshape(-1)

    up = tm_permute(kv, 0, 1, 0)
    down = tm_permute(kv, 0, -1, 0)
    kvs = [kv, tm_permute(kv, 0, 0, 1)]
    far_query = tm_permute(query, 1, 0, 0)
    for step in range(1, Z // 2 + 1):
        if step == 1:
            up, down, far_query, w_out_t = lax.optimization_barrier((up, down, far_query, w_out_t))
        elif step == 2:
            up, down, pair = lax.optimization_barrier((up, down, pair))
        elif step == 3:
            up, down = lax.optimization_barrier((up, down))
        else:
            up, east = lax.optimization_barrier((up, east))
        got = [up] if step == Z // 2 else [up, down]
        if step < Z // 2:
            up = tm_permute(up, 0, 1, 0)
        if step < Z // 2 - 1:
            down = tm_permute(down, 0, -1, 0)
        if step == 1:
            pair = jnp.stack([w_out_t, head_permute(w_out_t, 1, 0)])
        elif step == 2:
            east = head_permute(pair, 0, 1)
        for piece in got:
            kvs += [piece, tm_permute(piece, 0, 0, 1)]
    queries = jnp.concatenate([query, far_query], axis=0)

    send, keep, keep_lse = attention(signs, bases, slope, queries, kvs, 128 ** (-0.5) * LOG2E)
    send, keep, east, pair = lax.optimization_barrier((send, keep, east, pair))
    got = tm_permute(send, 1, 0, 0)
    weights = [pair, east, head_permute(pair, 0, -1), head_permute(east, 0, 1)]
    mixed = merge_halves(keep, keep_lse, got).reshape(YL * X, rows // (YL * X), 128)
    mixed = lax.all_to_all(mixed, "head", split_axis=0, concat_axis=0, tiled=True)
    place = lax.axis_index("head")
    turn, shift = jnp.array([0, 1] * X, jnp.int32), jnp.array([0, 0, 1, 1, 3, 3, 2, 2], jnp.int32)
    heads = (place // X + turn) % YL * X + (place + shift) % X
    return output_projection(heads, mixed, weights)


def solution(mesh):
    in_specs = (P("tm", None), P(), P(None, "tm", "head"), P("head"), P("head", "tm"))
    out_specs = P(("tm", "head"), None)
    return jax.shard_map(local, mesh=mesh, in_specs=in_specs, out_specs=out_specs, check_vma=False)
```
